32 devices in a mesh: ctx: 8 (over z, core), dp: 4 (over y, x).
Axes of the slice: x: 2, y: 2, z: 4, core: 2. Of those that a mesh axis runs over, the one named last changes fastest.
Arguments:
- projected: bfloat16 [8, 2, 64, 3, 8192], P('ctx', None, None, None, 'dp'), may hold values from -36 to 36, as said below
- filters: float32 [3, 7, 512], P(None, None, 'dp'), may hold values from -0.5 to 1.4, as said below
- gain: float32 [8192], P('dp'), may hold values from 0.5 to 1.5
- doc_lengths: int32 [4], replicated, may hold values from 1 to 320, 1024 in all
Outputs:
- mixed: bfloat16 [8, 2, 64, 8192], P('ctx', None, None, 'dp')
The draws below stay inside these ranges and needn't reach their ends.
Inputs may be any that keep to these rules, and one draw needn't show every extreme that they name: `doc_lengths`: each document holds 1 to 320 tokens, the longest exactly 320; the lengths sum to 1024. `projected`: entries are finite. `filters`: filter taps other than the last lie in -0.5 to 0.5; the last lies in 0.6 to 1.4.
All inputs are finite; a program needn't handle non-finite values.
Results may differ from the reference program's by a relative error of at most 0.004.
The reference program's roundings to bfloat16 on the way count: a program that leaves them out, or rounds other values in their place, can miss the bound.
Values may be sent and summed in bfloat16 or wider, within the bound.
A program may use at most 64 MiB of HBM per device.

```python
import math
import jax
import jax.numpy as jnp
import numpy as np
from jax import lax

D = 8192
HEADS = 64
HEAD_DIM = 128
GROUPS = 512
TAPS = 7
REACH = 5
STRETCH = 64
SEQ = 1024
DOCS = 4
N_CTX = 8


def draw_projected(key, part):
    shape = (N_CTX, 2, STRETCH, 3, D)
    base = jax.random.truncated_normal(key, -6.0, 6.0, shape, jnp.float32)
    channel = jnp.arange(D, dtype=jnp.float32) / (D - 1)
    ramp = jnp.exp(0.5 * jnp.log(3.0) * channel)
    multiplier = jnp.stack([jnp.ones((D,), jnp.float32), jnp.ones((D,), jnp.float32), ramp])
    return (base * multiplier).astype(jnp.bfloat16)


def draw_filters(key, part):
    shape = (3, TAPS, GROUPS)
    others = jax.random.uniform(jax.random.fold_in(key, 21), shape, jnp.float32, -0.5, 0.5)
    current = jax.random.uniform(jax.random.fold_in(key, 22), shape, jnp.float32, 0.6, 1.4)
    is_current = (jnp.arange(TAPS) == TAPS - 1)[None, :, None]
    return jnp.where(is_current, current, others)


def length_profile(amount, total, bound, skew):
    loads = [(1 << 20) // math.isqrt(rank ** skew) + 1 for rank in range(2, amount + 1)]
    spare, given = total - bound - (amount - 1), [1] * (amount - 1)
    while spare > 0:
        candidates = [i for i in range(amount - 1) if given[i] < bound]
        whole, left = sum([loads[i] for i in candidates]), spare
        for i in candidates:
            addition = min(bound - given[i], max(1, left * loads[i] // whole), spare)
            given[i] = given[i] + addition
            spare = spare - addition
    return np.array([bound] + given)


def uneven(own_key, count, total, bound, lean):
    if count == 2:
        one = jax.random.randint(own_key, (), max(1, total - bound), min(bound, total - 1) + 1)
        return jnp.stack([one, total - one])
    lengths = jnp.asarray(length_profile(count, total, bound, lean), jnp.int32)
    couples = (count - 1) // 2
    source_of, taker = lengths[1:1 + 2 * couples:2], lengths[2:2 + 2 * couples:2]
    margin = jnp.minimum(source_of - 1, bound - taker)
    passed = jax.random.randint(jax.random.fold_in(own_key, 1), (couples,), 0, 1 << 20) % (margin + 1)
    lengths = lengths.at[1:1 + 2 * couples:2].set(source_of - passed).at[2:2 + 2 * couples:2].set(taker + passed)
    return lengths[jax.random.permutation(jax.random.fold_in(own_key, 2), count)]


def setup_inputs(seed: int = 0) -> dict:
    arg_keys = jax.random.split(jax.random.key(seed), 5)
    projected = draw_projected(jax.random.fold_in(arg_keys[4], 71), 0)
    filters = draw_filters(jax.random.fold_in(arg_keys[4], 71), 0)
    gain = jnp.clip(1.0 + 0.1 * jax.random.normal(arg_keys[2], (D,), jnp.float32), 0.5, 1.5)
    doc_lengths = uneven(arg_keys[3], DOCS, SEQ, REACH * STRETCH, 2).astype(jnp.int32)
    return {"projected": projected, "filters": filters, "gain": gain, "doc_lengths": doc_lengths}


def reference(projected, filters, gain, doc_lengths):
    doc_ends = jnp.cumsum(doc_lengths).astype(jnp.int32)
    wide_filters = jnp.repeat(filters, D // GROUPS, axis=2)
    tap_weights = jnp.transpose(wide_filters, (1, 0, 2))
    rim_width = TAPS - 1
    window_blocks = REACH + 1

    def block_rows(block_id):
        valid = block_id >= 0
        clipped = jnp.maximum(block_id, 0).astype(jnp.int32)
        slot_index = jnp.where(clipped < N_CTX, clipped, 2 * N_CTX - 1 - clipped).astype(jnp.int32)
        half_index = jnp.where(clipped < N_CTX, 0, 1).astype(jnp.int32)
        rows = projected[slot_index, half_index]
        return jnp.where(valid, rows, jnp.zeros_like(rows))

    def doc_of(positions):
        return lax.optimization_barrier(jnp.sum((doc_ends[None, :] <= positions[:, None]).astype(jnp.int32), axis=1))

    def conv_block(block_id):
        older = block_rows(block_id - 1)[STRETCH - rim_width:]
        window_rows = jnp.concatenate([older, block_rows(block_id)], axis=0)
        summed = jnp.zeros((STRETCH, 3, D), jnp.float32)
        for tap_index in range(TAPS):
            summed = summed + window_rows[tap_index:tap_index + STRETCH].astype(jnp.float32) * tap_weights[tap_index]
        return summed.astype(jnp.bfloat16)
    conv_all = lax.map(conv_block, jnp.arange(2 * N_CTX, dtype=jnp.int32))

    def one_block(block_id):
        first = jnp.maximum(block_id - REACH, 0).astype(jnp.int32)
        window = lax.dynamic_slice_in_dim(conv_all, first, window_blocks, 0)
        window = window.reshape(window_blocks * STRETCH, 3, D)
        own = lax.dynamic_index_in_dim(conv_all, block_id, 0, keepdims=False)
        queries = own[:, 0].astype(jnp.float32).reshape(STRETCH, HEADS, HEAD_DIM)
        keys_all = window[:, 1].astype(jnp.float32).reshape(window_blocks * STRETCH, HEADS, HEAD_DIM)
        values_all = window[:, 2].astype(jnp.float32).reshape(window_blocks * STRETCH, HEADS, HEAD_DIM)
        query_pos = block_id * STRETCH + jnp.arange(STRETCH, dtype=jnp.int32)
        key_pos = first * STRETCH + jnp.arange(window_blocks * STRETCH, dtype=jnp.int32)
        allowed = (key_pos[None, :] <= query_pos[:, None]) & (key_pos[None, :] >= 0)
        allowed = allowed & (doc_of(query_pos)[:, None] == doc_of(key_pos)[None, :])
        scores = jnp.einsum('qhd,khd->hqk', queries, keys_all) * HEAD_DIM ** (-0.5)
        scores = jnp.where(allowed[None], scores, -1e+30)
        row_max = lax.optimization_barrier(jnp.max(scores, axis=-1, keepdims=True))
        exp_terms = jnp.exp(scores - row_max)
        row_total = lax.optimization_barrier(jnp.sum(exp_terms, axis=-1, keepdims=True))
        rounded = lax.optimization_barrier(exp_terms.astype(jnp.bfloat16))
        weights = rounded.astype(jnp.float32)
        attended = jnp.einsum('hqk,khd->qhd', weights, values_all) / jnp.transpose(row_total, (1, 0, 2))
        flat = attended.reshape(STRETCH, D)
        squares = lax.optimization_barrier(jnp.sum(flat * flat, axis=-1, keepdims=True))
        return (flat * lax.rsqrt(squares / D + 1e-06) * gain).astype(jnp.bfloat16)
    results = lax.map(one_block, jnp.arange(2 * N_CTX, dtype=jnp.int32))
    return jnp.stack([results[:N_CTX], results[::-1][:N_CTX]], axis=1)
```

```python
import functools

import jax
import jax.numpy as jnp
from jax import lax
from jax.experimental import pallas as pl
from jax.experimental.pallas import tpu as pltpu
from jax.sharding import PartitionSpec as P

HEAD_DIM = 128
REACH = 5
RIM = 8
HEAD_ROWS = 16
PAIRS = (REACH + 1) // 2
MESH = pl.DeviceIdType.MESH


def kernel(
    n_ctx,
    n_dp,
    x_ref,
    f_ref,
    gain_ref,
    docs_ref,
    out_ref,
    xs,
    xf,
    fw,
    halo,
    qb,
    kv,
    run_max,
    run_total,
    acc,
    squares,
    inv_norm,
    sq_own,
    sq_peer,
    starts,
    load_sem,
    halo_send,
    halo_recv,
    kv_send,
    kv_recv,
    sq_send,
    sq_recv,
):
    rows = xs.shape[2]
    width = xs.shape[3]
    groups = kv.shape[1]
    group_width = kv.shape[4]
    group_heads = group_width // HEAD_DIM
    taps = f_ref.shape[1]
    place = lax.axis_index("ctx")
    lane = lax.axis_index("dp")
    right = lax.rem(place + 1, n_ctx)
    left = lax.rem(place + n_ctx - 1, n_ctx)
    has_left = place > 0
    has_right = place < n_ctx - 1
    is_last = place == n_ctx - 1

    load_kv = [
        pltpu.make_async_copy(x_ref.at[b, pl.ds(1, 2)], xs.at[b, pl.ds(1, 2)], load_sem.at[b])
        for b in range(2)
    ]
    load_q = [
        pltpu.make_async_copy(x_ref.at[b, 0], xs.at[b, 0], load_sem.at[2 + b]) for b in range(2)
    ]
    for copy in load_kv + load_q:
        copy.start()

    barrier = pltpu.get_barrier_semaphore()

    @pl.when(has_left)
    def _():
        pl.semaphore_signal(barrier, inc=1, device_id={"ctx": left}, device_id_type=MESH)

    @pl.when(has_right)
    def _():
        pl.semaphore_signal(barrier, inc=1, device_id={"ctx": right}, device_id_type=MESH)

    for step in range(1, n_dp):
        peer = lax.rem(lane + step, n_dp)
        pl.semaphore_signal(barrier, inc=1, device_id={"dp": peer}, device_id_type=MESH)

    def rim(b, source, target):
        return pltpu.make_async_remote_copy(
            src_ref=x_ref.at[source, :, pl.ds(rows - RIM, RIM), :],
            dst_ref=halo.at[b],
            send_sem=halo_send.at[b],
            recv_sem=halo_recv.at[b],
            device_id={"ctx": target},
            device_id_type=MESH,
        )

    rim_lower = rim(0, 0, right)
    rim_upper = rim(1, 1, left)
    rim_fold = pltpu.make_async_copy(
        x_ref.at[0, :, pl.ds(rows - RIM, RIM), :], halo.at[1], halo_recv.at[1]
    )
    pl.semaphore_wait(barrier, n_dp - 1 + has_left.astype(jnp.int32) + has_right.astype(jnp.int32))

    @pl.when(has_right)
    def _():
        rim_lower.start()

    @pl.when(has_left)
    def _():
        rim_upper.start()

    @pl.when(is_last)
    def _():
        rim_fold.start()

    spread_shape = (f_ref.shape[2], HEAD_DIM)
    spread_row = lax.broadcasted_iota(jnp.int32, spread_shape, 0)
    spread_col = lax.broadcasted_iota(jnp.int32, spread_shape, 1)
    group_size = width // f_ref.shape[2]
    for m in range(3):
        taps_m = f_ref[m]
        for h in range(width // HEAD_DIM):
            first = h * HEAD_DIM
            hot = (spread_row * group_size <= first + spread_col) & (
                first + spread_col < (spread_row + 1) * group_size
            )
            fw[m, pl.ds(0, taps), pl.ds(first, HEAD_DIM)] = jnp.dot(
                taps_m,
                jnp.where(hot, 1.0, 0.0).astype(jnp.float32),
                precision=lax.Precision.HIGHEST,
                preferred_element_type=jnp.float32,
            )

    for d in range(1, REACH + 1):

        @pl.when(place < d)
        def _():
            def clear(g, carry):
                kv[0, g, :, pl.ds(d * rows, rows), :] = jnp.zeros(
                    (2, rows, group_width), jnp.bfloat16
                )
                return carry

            lax.fori_loop(0, groups, clear, 0)

    @pl.when(place == 0)
    def _():
        halo[0] = jnp.zeros(halo.shape[1:], jnp.bfloat16)

    offsets = lax.broadcasted_iota(jnp.int32, (rows, HEAD_DIM), 0)
    block_start = [place * rows, (2 * n_ctx - 1 - place) * rows]
    for b in range(2):
        positions = block_start[b] + offsets

        def advance(k, carry):
            begin, end = carry
            end = end + docs_ref[k]
            return jnp.where(positions >= end, end, begin), end

        begin, _ = lax.fori_loop(
            0, docs_ref.shape[0], advance, (jnp.zeros_like(positions), jnp.int32(0))
        )
        starts[b] = begin

    def convolved(b, m, lanes, first, count):
        total = None
        for s in range(taps):
            term = fw[m, pl.ds(s, 1), lanes] * xf[b, m, pl.ds(first + RIM - taps + 1 + s, count), lanes]
            total = term if total is None else total + term
        return total.astype(jnp.bfloat16)

    def channel(g, hl):
        return pl.ds(pl.multiple_of(g * group_width + hl * HEAD_DIM, HEAD_DIM), HEAD_DIM)

    def inner(hl):
        return pl.ds(hl * HEAD_DIM, HEAD_DIM)

    for copy in load_kv:
        copy.wait()

    def body_rows(i, carry):
        b, g = lax.div(i, groups), lax.rem(i, groups)
        for m in (1, 2):
            for hl in range(group_heads):
                lanes = channel(g, hl)
                xf[b, m, pl.ds(RIM, rows), lanes] = xs[b, m, :, lanes].astype(jnp.float32)
            for hl in range(group_heads):
                kv[b, g, m - 1, pl.ds(HEAD_ROWS, rows - HEAD_ROWS), inner(hl)] = convolved(
                    b, m, channel(g, hl), HEAD_ROWS, rows - HEAD_ROWS
                )
        return carry

    lax.fori_loop(0, 2 * groups, body_rows, 0)

    @pl.when(has_left)
    def _():
        rim_lower.wait_recv()

    @pl.when(has_right)
    def _():
        rim_upper.wait_recv()

    @pl.when(is_last)
    def _():
        rim_fold.wait()

    def slot(b, g, d):
        return kv.at[b, g, :, pl.ds(d * rows, rows), :]

    def moved(b, g, d, target):
        return pltpu.make_async_remote_copy(
            src_ref=slot(b, g, d - 1),
            dst_ref=slot(b, g, d),
            send_sem=kv_send.at[b, d - 1, g],
            recv_sem=kv_recv.at[b, d - 1, g],
            device_id={"ctx": target},
            device_id_type=MESH,
        )

    def folded(g, d):
        return pltpu.make_async_copy(slot(0, g, d - 1), slot(1, g, d), kv_recv.at[1, d - 1, g])

    def lower_sends(d):
        return has_right & (place + 1 >= d)

    def launch(g, d):
        @pl.when(has_left)
        def _():
            moved(1, g, d, left).start()

        @pl.when(lower_sends(d))
        def _():
            moved(0, g, d, right).start()

        @pl.when(is_last)
        def _():
            folded(g, d).start()

    def arrive(g, d):
        @pl.when(place >= d)
        def _():
            moved(0, g, d, right).wait_recv()

        @pl.when(has_right)
        def _():
            moved(1, g, d, left).wait_recv()

        @pl.when(is_last)
        def _():
            folded(g, d).wait()

    def first_rows(g, carry):
        for b in range(2):
            for m in (1, 2):
                for hl in range(group_heads):
                    lanes = channel(g, hl)
                    xf[b, m, pl.ds(0, RIM), lanes] = halo[b, m, :, lanes].astype(jnp.float32)
                    kv[b, g, m - 1, pl.ds(0, HEAD_ROWS), inner(hl)] = convolved(
                        b, m, lanes, 0, HEAD_ROWS
                    )
        launch(g, 1)
        return carry

    lax.fori_loop(0, groups, first_rows, 0)

    for copy in load_q:
        copy.wait()

    def query_rows(i, carry):
        b, g = lax.div(i, groups), lax.rem(i, groups)
        for hl in range(group_heads):
            lanes = channel(g, hl)
            xf[b, 0, pl.ds(0, RIM), lanes] = halo[b, 0, :, lanes].astype(jnp.float32)
            xf[b, 0, pl.ds(RIM, rows), lanes] = xs[b, 0, :, lanes].astype(jnp.float32)
        for hl in range(group_heads):
            qb[b, g, :, inner(hl)] = convolved(b, 0, channel(g, hl), 0, rows)
        return carry

    lax.fori_loop(0, 2 * groups, query_rows, 0)

    key_lane = lax.broadcasted_iota(jnp.int32, (rows, HEAD_DIM), 1)
    key_offset = jnp.where(key_lane >= rows, key_lane - 2 * rows, key_lane)
    span = 2 * rows

    def attend(pair, b, g):
        block = place * rows if b == 0 else (2 * n_ctx - 1 - place) * rows
        key_pos = key_offset + (block - pair * span)
        allowed = (key_pos >= starts[b]) & (key_pos <= block + offsets)
        for hl in range(group_heads):
            lanes = inner(hl)
            query = qb[b, g, :, lanes]
            key = kv[b, g, 0, pl.ds(pair * span, span), lanes]
            value = kv[b, g, 1, pl.ds(pair * span, span), lanes]
            scores = lax.dot_general(
                query, key, (((1,), (1,)), ((), ())), preferred_element_type=jnp.float32
            ) * HEAD_DIM ** (-0.5)
            scores = jnp.where(allowed, scores, -1e30)
            top = jnp.max(scores, axis=1, keepdims=True)
            if pair > 0:
                before = run_max[b, g, hl]
                top = jnp.maximum(before, top)
            expo = jnp.exp(scores - top)
            total = jnp.sum(expo, axis=1, keepdims=True)
            update = jnp.dot(
                expo.astype(jnp.bfloat16), value, preferred_element_type=jnp.float32
            )
            if pair > 0:
                rescale = jnp.exp(before - top)
                total = run_total[b, g, hl] * rescale + total
                update = acc[b, g, :, lanes] * rescale + update
            if pair < PAIRS - 1:
                run_max[b, g, hl] = jnp.broadcast_to(top, (rows, HEAD_DIM))
                run_total[b, g, hl] = jnp.broadcast_to(total, (rows, HEAD_DIM))
                acc[b, g, :, lanes] = update
            else:
                attended = update / total
                acc[b, g, :, lanes] = attended
                squares[pl.ds(b * rows, rows), :] += attended * attended

    squares[...] = jnp.zeros_like(squares)
    for d in range(1, REACH):

        def relay(g, carry):
            arrive(g, d)
            launch(g, d + 1)
            return carry

        lax.fori_loop(0, groups, relay, 0)
        if d % 2 == 1:

            def work(g, carry):
                for b in range(2):
                    attend(d // 2, b, g)
                return carry

            lax.fori_loop(0, groups, work, 0)

    def finish(g, carry):
        arrive(g, REACH)
        for b in range(2):
            attend(PAIRS - 1, b, g)
        return carry

    lax.fori_loop(0, groups, finish, 0)

    row = jnp.sum(jnp.transpose(squares[...]), axis=0, keepdims=True)
    sq_own[...] = jnp.broadcast_to(row, sq_own.shape)
    shares = []
    for step in range(1, n_dp):
        share = pltpu.make_async_remote_copy(
            src_ref=sq_own,
            dst_ref=sq_peer.at[step - 1],
            send_sem=sq_send.at[step - 1],
            recv_sem=sq_recv.at[step - 1],
            device_id={"dp": lax.rem(lane + step, n_dp)},
            device_id_type=MESH,
        )
        share.start()
        shares.append(share)

    @pl.when(has_right)
    def _():
        rim_lower.wait_send()

    @pl.when(has_left)
    def _():
        rim_upper.wait_send()

    for d in range(1, REACH + 1):

        def drain(g, carry):
            @pl.when(has_left)
            def _():
                moved(1, g, d, left).wait_send()

            @pl.when(lower_sends(d))
            def _():
                moved(0, g, d, right).wait_send()

            return carry

        lax.fori_loop(0, groups, drain, 0)

    whole = sq_own[...]
    for step in range(1, n_dp):
        shares[step - 1].wait()
        whole = whole + sq_peer[step - 1]
    inverse = lax.rsqrt(whole / (width * n_dp) + 1e-06)
    inv_norm[...] = jnp.transpose(jnp.broadcast_to(inverse[0:1], inv_norm.shape))

    def norm(g, carry):
        for b in range(2):
            factor = inv_norm[pl.ds(b * rows, rows), :]
            for hl in range(group_heads):
                lanes = channel(g, hl)
                out_ref[b, :, lanes] = (
                    acc[b, g, :, inner(hl)] * factor * gain_ref[:, lanes]
                ).astype(jnp.bfloat16)
        return carry

    lax.fori_loop(0, groups, norm, 0)


def local(n_ctx, n_dp, projected, filters, gain, doc_lengths):
    blocks = jnp.transpose(projected[0], (0, 2, 1, 3))
    rows, width = blocks.shape[2], blocks.shape[3]
    group_width = min(width, 4 * HEAD_DIM)
    groups = width // group_width
    group_heads = group_width // HEAD_DIM
    vmem = pl.BlockSpec(memory_space=pltpu.VMEM)
    out = pl.pallas_call(
        functools.partial(kernel, n_ctx, n_dp),
        out_shape=jax.ShapeDtypeStruct((2, rows, width), jnp.bfloat16),
        in_specs=[
            pl.BlockSpec(memory_space=pl.ANY),
            vmem,
            vmem,
            pl.BlockSpec(memory_space=pltpu.SMEM),
        ],
        out_specs=vmem,
        scratch_shapes=[
            pltpu.VMEM((2, 3, rows, width), jnp.bfloat16),
            pltpu.VMEM((2, 3, RIM + rows, width), jnp.float32),
            pltpu.VMEM((3, 8, width), jnp.float32),
            pltpu.VMEM((2, 3, RIM, width), jnp.bfloat16),
            pltpu.VMEM((2, groups, rows, group_width), jnp.bfloat16),
            pltpu.VMEM((2, groups, 2, (REACH + 1) * rows, group_width), jnp.bfloat16),
            pltpu.VMEM((2, groups, group_heads, rows, HEAD_DIM), jnp.float32),
            pltpu.VMEM((2, groups, group_heads, rows, HEAD_DIM), jnp.float32),
            pltpu.VMEM((2, groups, rows, group_width), jnp.float32),
            pltpu.VMEM((2 * rows, HEAD_DIM), jnp.float32),
            pltpu.VMEM((2 * rows, HEAD_DIM), jnp.float32),
            pltpu.VMEM((8, 2 * rows), jnp.float32),
            pltpu.VMEM((n_dp - 1, 8, 2 * rows), jnp.float32),
            pltpu.VMEM((2, rows, HEAD_DIM), jnp.int32),
            pltpu.SemaphoreType.DMA((4,)),
            pltpu.SemaphoreType.DMA((2,)),
            pltpu.SemaphoreType.DMA((2,)),
            pltpu.SemaphoreType.DMA((2, REACH, groups)),
            pltpu.SemaphoreType.DMA((2, REACH, groups)),
            pltpu.SemaphoreType.DMA((n_dp - 1,)),
            pltpu.SemaphoreType.DMA((n_dp - 1,)),
        ],
        compiler_params=pltpu.CompilerParams(
            collective_id=0, has_side_effects=True, vmem_limit_bytes=48 * 1024 * 1024
        ),
    )(blocks, filters, gain[None, :], doc_lengths)
    return out[None]


def solution(mesh):
    in_specs = (P("ctx", None, None, None, "dp"), P(None, None, "dp"), P("dp"), P())
    out_specs = P("ctx", None, None, "dp")
    return jax.shard_map(
        functools.partial(local, mesh.shape["ctx"], mesh.shape["dp"]),
        mesh=mesh,
        in_specs=in_specs,
        out_specs=out_specs,
        check_vma=False,
    )
```

```python
import functools
import math

import jax
import jax.numpy as jnp
from jax import lax
from jax.experimental import pallas as pl
from jax.experimental.pallas import tpu as pltpu
from jax.sharding import PartitionSpec as P

HEAD_DIM = 128
REACH = 5
RIM = 8
HEAD_ROWS = 16
PAIRS = (REACH + 1) // 2
LOG2_SCALE = HEAD_DIM ** (-0.5) * math.log2(math.e)
MESH = pl.DeviceIdType.MESH


def kernel(
    n_ctx,
    n_dp,
    x_ref,
    f_hbm,
    gain_hbm,
    docs_hbm,
    out_ref,
    f_ref,
    gain_ref,
    docs_ref,
    parts,
    xs,
    xf,
    fw,
    halo,
    qb,
    kv,
    run_max,
    run_total,
    acc,
    squares,
    inv_norm,
    sq_own,
    sq_peer,
    starts,
    load_sem,
    halo_send,
    halo_recv,
    kv_send,
    kv_recv,
    sq_send,
    sq_recv,
):
    rows = xs.shape[2]
    width = xs.shape[3]
    groups = kv.shape[1]
    group_width = kv.shape[4]
    group_heads = group_width // HEAD_DIM
    taps = f_ref.shape[1]
    place = lax.axis_index("ctx")
    lane = lax.axis_index("dp")
    right = lax.rem(place + 1, n_ctx)
    left = lax.rem(place + n_ctx - 1, n_ctx)
    has_left = place > 0
    has_right = place < n_ctx - 1
    is_last = place == n_ctx - 1

    load_kv = [
        pltpu.make_async_copy(x_ref.at[b, pl.ds(1, 2)], xs.at[b, pl.ds(1, 2)], load_sem.at[b])
        for b in range(2)
    ]
    load_q = [
        pltpu.make_async_copy(x_ref.at[b, 0], xs.at[b, 0], load_sem.at[2 + b]) for b in range(2)
    ]
    load_small = [
        pltpu.make_async_copy(f_hbm, f_ref, load_sem.at[4]),
        pltpu.make_async_copy(docs_hbm, docs_ref, load_sem.at[5]),
        pltpu.make_async_copy(gain_hbm, gain_ref, load_sem.at[6]),
    ]
    for copy in load_small + load_kv + load_q:
        copy.start()

    barrier = pltpu.get_barrier_semaphore()

    @pl.when(has_left)
    def _():
        pl.semaphore_signal(barrier, inc=1, device_id={"ctx": left}, device_id_type=MESH)

    @pl.when(has_right)
    def _():
        pl.semaphore_signal(barrier, inc=1, device_id={"ctx": right}, device_id_type=MESH)

    for step in range(1, n_dp):
        peer = lax.rem(lane + step, n_dp)
        pl.semaphore_signal(barrier, inc=1, device_id={"dp": peer}, device_id_type=MESH)

    def rim(b, source, target):
        return pltpu.make_async_remote_copy(
            src_ref=x_ref.at[source, :, pl.ds(rows - RIM, RIM), :],
            dst_ref=halo.at[b],
            send_sem=halo_send.at[b],
            recv_sem=halo_recv.at[b],
            device_id={"ctx": target},
            device_id_type=MESH,
        )

    rim_lower = rim(0, 0, right)
    rim_upper = rim(1, 1, left)
    rim_fold = pltpu.make_async_copy(
        x_ref.at[0, :, pl.ds(rows - RIM, RIM), :], halo.at[1], halo_recv.at[1]
    )
    spread_shape = (f_ref.shape[2], HEAD_DIM)
    spread_row = lax.broadcasted_iota(jnp.int32, spread_shape, 0)
    spread_col = lax.broadcasted_iota(jnp.int32, spread_shape, 1)
    group_size = width // f_ref.shape[2]
    parts[...] = jnp.zeros_like(parts)
    load_small[0].wait()
    for m in range(3):
        left_over = f_ref[m]
        for part in range(3):
            piece = left_over.astype(jnp.bfloat16).astype(jnp.float32)
            parts[3 * part + m, pl.ds(0, taps), :] = piece
            left_over = left_over - piece
    split = parts[...].reshape(72, f_ref.shape[2]).astype(jnp.bfloat16)
    for h in range(width // HEAD_DIM):
        first = h * HEAD_DIM
        hot = (spread_row * group_size <= first + spread_col) & (
            first + spread_col < (spread_row + 1) * group_size
        )
        spread = jnp.dot(
            split,
            jnp.where(hot, 1.0, 0.0).astype(jnp.bfloat16),
            preferred_element_type=jnp.float32,
        ).reshape(9, 8, HEAD_DIM)
        for m in range(3):
            fw[m, :, pl.ds(first, HEAD_DIM)] = (spread[m] + spread[3 + m]) + spread[6 + m]

    pl.semaphore_wait(barrier, n_dp - 1 + has_left.astype(jnp.int32) + has_right.astype(jnp.int32))

    @pl.when(has_right)
    def _():
        rim_lower.start()

    @pl.when(has_left)
    def _():
        rim_upper.start()

    @pl.when(is_last)
    def _():
        rim_fold.start()

    def convolved(b, m, lanes, first, count):
        total = None
        for s in range(taps):
            term = fw[m, pl.ds(s, 1), lanes] * xf[b, m, pl.ds(first + RIM - taps + 1 + s, count), lanes]
            total = term if total is None else total + term
        return total.astype(jnp.bfloat16)

    def channel(g, hl):
        return pl.ds(pl.multiple_of(g * group_width + hl * HEAD_DIM, HEAD_DIM), HEAD_DIM)

    def inner(hl):
        return pl.ds(hl * HEAD_DIM, HEAD_DIM)

    def slot(b, g, d, first=0, count=rows):
        return kv.at[b, g, :, pl.ds(d * rows + first, count), :]

    def moved(b, g, d, target, first=0, count=rows):
        return pltpu.make_async_remote_copy(
            src_ref=slot(b, g, d - 1, first, count),
            dst_ref=slot(b, g, d, first, count),
            send_sem=kv_send.at[b, d - 1, g],
            recv_sem=kv_recv.at[b, d - 1, g],
            device_id={"ctx": target},
            device_id_type=MESH,
        )

    def folded(g, d):
        return pltpu.make_async_copy(slot(0, g, d - 1), slot(1, g, d), kv_recv.at[1, d - 1, g])

    def lower_sends(d):
        return has_right & (place + 1 >= d)

    def launch(g, d, first=0, count=rows):
        @pl.when(has_left)
        def _():
            moved(1, g, d, left, first, count).start()

        @pl.when(lower_sends(d))
        def _():
            moved(0, g, d, right, first, count).start()

        if first == 0:

            @pl.when(is_last)
            def _():
                folded(g, d).start()

    def arrive(g, d):
        @pl.when(place >= d)
        def _():
            moved(0, g, d, right).wait_recv()

        @pl.when(has_right)
        def _():
            moved(1, g, d, left).wait_recv()

        @pl.when(is_last)
        def _():
            folded(g, d).wait()

    for copy in load_kv:
        copy.wait()

    def body_rows(g, carry):
        for b in range(2):
            for m in (1, 2):
                for hl in range(group_heads):
                    lanes = channel(g, hl)
                    xf[b, m, pl.ds(RIM, rows), lanes] = xs[b, m, :, lanes].astype(jnp.float32)
                for hl in range(group_heads):
                    kv[b, g, m - 1, pl.ds(HEAD_ROWS, rows - HEAD_ROWS), inner(hl)] = convolved(
                        b, m, channel(g, hl), HEAD_ROWS, rows - HEAD_ROWS
                    )
        launch(g, 1, HEAD_ROWS, rows - HEAD_ROWS)
        return carry

    lax.fori_loop(0, groups, body_rows, 0)

    @pl.when(place == 0)
    def _():
        halo[0] = jnp.zeros(halo.shape[1:], jnp.bfloat16)

    @pl.when(has_left)
    def _():
        rim_lower.wait_recv()

    @pl.when(has_right)
    def _():
        rim_upper.wait_recv()

    @pl.when(is_last)
    def _():
        rim_fold.wait()

    def first_rows(g, carry):
        for b in range(2):
            for m in (1, 2):
                for hl in range(group_heads):
                    lanes = channel(g, hl)
                    xf[b, m, pl.ds(0, RIM), lanes] = halo[b, m, :, lanes].astype(jnp.float32)
                    kv[b, g, m - 1, pl.ds(0, HEAD_ROWS), inner(hl)] = convolved(
                        b, m, lanes, 0, HEAD_ROWS
                    )
        launch(g, 1, 0, HEAD_ROWS)
        return carry

    lax.fori_loop(0, groups, first_rows, 0)

    for d in range(1, REACH + 1):

        @pl.when(place < d)
        def _():
            def clear(g, carry):
                kv[0, g, :, pl.ds(d * rows, rows), :] = jnp.zeros(
                    (2, rows, group_width), jnp.bfloat16
                )
                return carry

            lax.fori_loop(0, groups, clear, 0)

    load_small[1].wait()

    offsets = lax.broadcasted_iota(jnp.int32, (rows, HEAD_DIM), 0)
    block_start = [place * rows, (2 * n_ctx - 1 - place) * rows]
    for b in range(2):
        positions = block_start[b] + offsets

        def advance(k, carry):
            begin, end = carry
            end = end + docs_ref[k]
            return jnp.where(positions >= end, end, begin), end

        begin, _ = lax.fori_loop(
            0, docs_ref.shape[0], advance, (jnp.zeros_like(positions), jnp.int32(0))
        )
        starts[b] = begin

    for copy in load_q:
        copy.wait()

    def query_rows(i, carry):
        b, g = lax.div(i, groups), lax.rem(i, groups)
        for hl in range(group_heads):
            lanes = channel(g, hl)
            xf[b, 0, pl.ds(0, RIM), lanes] = halo[b, 0, :, lanes].astype(jnp.float32)
            xf[b, 0, pl.ds(RIM, rows), lanes] = xs[b, 0, :, lanes].astype(jnp.float32)
        for hl in range(group_heads):
            qb[b, g, :, inner(hl)] = convolved(b, 0, channel(g, hl), 0, rows)
        return carry

    lax.fori_loop(0, 2 * groups, query_rows, 0)

    key_lane = lax.broadcasted_iota(jnp.int32, (rows, HEAD_DIM), 1)
    key_offset = jnp.where(key_lane >= rows, key_lane - 2 * rows, key_lane)
    span = 2 * rows

    def attend(pair, b, g):
        block = place * rows if b == 0 else (2 * n_ctx - 1 - place) * rows
        key_pos = key_offset + (block - pair * span)
        allowed = (key_pos >= starts[b]) & (key_pos <= block + offsets)
        heads = range(group_heads)
        keys = pl.ds(pair * span, span)
        scores = [
            lax.dot_general(
                qb[b, g, :, inner(hl)],
                kv[b, g, 0, keys, inner(hl)],
                (((1,), (1,)), ((), ())),
                preferred_element_type=jnp.float32,
            )
            for hl in heads
        ]
        scores = [jnp.where(allowed, score * LOG2_SCALE, -1e30) for score in scores]
        tops = [jnp.max(score, axis=1, keepdims=True) for score in scores]
        if pair > 0:
            before = [run_max[b, g, hl] for hl in heads]
            tops = [jnp.maximum(old, top) for old, top in zip(before, tops)]
        expos = [jnp.exp2(score - top) for score, top in zip(scores, tops)]
        updates = [
            jnp.dot(
                expos[hl].astype(jnp.bfloat16),
                kv[b, g, 1, keys, inner(hl)],
                preferred_element_type=jnp.float32,
            )
            for hl in heads
        ]
        totals = [jnp.sum(expo, axis=1, keepdims=True) for expo in expos]
        if pair > 0:
            rescales = [jnp.exp2(old - top) for old, top in zip(before, tops)]
            totals = [run_total[b, g, hl] * rescales[hl] + totals[hl] for hl in heads]
            updates = [acc[b, g, :, inner(hl)] * rescales[hl] + updates[hl] for hl in heads]
        if pair < PAIRS - 1:
            for hl in heads:
                run_max[b, g, hl] = jnp.broadcast_to(tops[hl], (rows, HEAD_DIM))
                run_total[b, g, hl] = jnp.broadcast_to(totals[hl], (rows, HEAD_DIM))
                acc[b, g, :, inner(hl)] = updates[hl]
        else:
            energy = squares[pl.ds(b * rows, rows), :]
            for hl in heads:
                attended = updates[hl] / totals[hl]
                acc[b, g, :, inner(hl)] = attended
                energy = energy + attended * attended
            squares[pl.ds(b * rows, rows), :] = energy

    squares[...] = jnp.zeros_like(squares)
    work = {2: ((0, 0),), 3: ((0, 1),), 4: ((1, 0), (1, 1))}
    for d in range(1, REACH):

        def relay(g, carry):
            arrive(g, d)
            launch(g, d + 1)
            for pair, b in work.get(d, ()):
                attend(pair, b, g)
            return carry

        lax.fori_loop(0, groups, relay, 0)

    def finish(g, carry):
        arrive(g, REACH)
        for b in range(2):
            attend(PAIRS - 1, b, g)
        return carry

    lax.fori_loop(0, groups, finish, 0)

    row = jnp.sum(jnp.transpose(squares[...]), axis=0, keepdims=True)
    sq_own[...] = jnp.broadcast_to(row, sq_own.shape)
    shares = []
    for step in range(1, n_dp):
        share = pltpu.make_async_remote_copy(
            src_ref=sq_own,
            dst_ref=sq_peer.at[step - 1],
            send_sem=sq_send.at[step - 1],
            recv_sem=sq_recv.at[step - 1],
            device_id={"dp": lax.rem(lane + step, n_dp)},
            device_id_type=MESH,
        )
        share.start()
        shares.append(share)

    @pl.when(has_right)
    def _():
        rim_lower.wait_send()

    @pl.when(has_left)
    def _():
        rim_upper.wait_send()

    for d in range(1, REACH + 1):

        def drain(g, carry):
            @pl.when(has_left)
            def _():
                moved(1, g, d, left).wait_send()

            @pl.when(lower_sends(d))
            def _():
                moved(0, g, d, right).wait_send()

            return carry

        lax.fori_loop(0, groups, drain, 0)

    whole = sq_own[...]
    for step in range(1, n_dp):
        shares[step - 1].wait()
        whole = whole + sq_peer[step - 1]
    inverse = lax.rsqrt(whole / (width * n_dp) + 1e-06)
    inv_norm[...] = jnp.transpose(jnp.broadcast_to(inverse[0:1], inv_norm.shape))

    load_small[2].wait()

    def norm(g, carry):
        for b in range(2):
            factor = inv_norm[pl.ds(b * rows, rows), :]
            for hl in range(group_heads):
                lanes = channel(g, hl)
                out_ref[b, :, lanes] = (
                    acc[b, g, :, inner(hl)] * factor * gain_ref[:, lanes]
                ).astype(jnp.bfloat16)
        return carry

    lax.fori_loop(0, groups, norm, 0)


def local(n_ctx, n_dp, projected, filters, gain, doc_lengths):
    blocks = jnp.transpose(projected[0], (0, 2, 1, 3))
    rows, width = blocks.shape[2], blocks.shape[3]
    group_width = min(width, 4 * HEAD_DIM)
    groups = width // group_width
    group_heads = group_width // HEAD_DIM
    vmem = pl.BlockSpec(memory_space=pltpu.VMEM)
    out = pl.pallas_call(
        functools.partial(kernel, n_ctx, n_dp),
        out_shape=jax.ShapeDtypeStruct((2, rows, width), jnp.bfloat16),
        in_specs=[
            pl.BlockSpec(memory_space=pltpu.HBM),
            pl.BlockSpec(memory_space=pltpu.HBM),
            pl.BlockSpec(memory_space=pltpu.HBM),
            pl.BlockSpec(memory_space=pltpu.HBM),
        ],
        out_specs=vmem,
        scratch_shapes=[
            pltpu.VMEM(filters.shape, jnp.float32),
            pltpu.VMEM((1, width), jnp.float32),
            pltpu.SMEM(doc_lengths.shape, jnp.int32),
            pltpu.VMEM((9, 8, filters.shape[2]), jnp.float32),
            pltpu.VMEM((2, 3, rows, width), jnp.bfloat16),
            pltpu.VMEM((2, 3, RIM + rows, width), jnp.float32),
            pltpu.VMEM((3, 8, width), jnp.float32),
            pltpu.VMEM((2, 3, RIM, width), jnp.bfloat16),
            pltpu.VMEM((2, groups, rows, group_width), jnp.bfloat16),
            pltpu.VMEM((2, groups, 2, (REACH + 1) * rows, group_width), jnp.bfloat16),
            pltpu.VMEM((2, groups, group_heads, rows, HEAD_DIM), jnp.float32),
            pltpu.VMEM((2, groups, group_heads, rows, HEAD_DIM), jnp.float32),
            pltpu.VMEM((2, groups, rows, group_width), jnp.float32),
            pltpu.VMEM((2 * rows, HEAD_DIM), jnp.float32),
            pltpu.VMEM((2 * rows, HEAD_DIM), jnp.float32),
            pltpu.VMEM((8, 2 * rows), jnp.float32),
            pltpu.VMEM((n_dp - 1, 8, 2 * rows), jnp.float32),
            pltpu.VMEM((2, rows, HEAD_DIM), jnp.int32),
            pltpu.SemaphoreType.DMA((7,)),
            pltpu.SemaphoreType.DMA((2,)),
            pltpu.SemaphoreType.DMA((2,)),
            pltpu.SemaphoreType.DMA((2, REACH, groups)),
            pltpu.SemaphoreType.DMA((2, REACH, groups)),
            pltpu.SemaphoreType.DMA((n_dp - 1,)),
            pltpu.SemaphoreType.DMA((n_dp - 1,)),
        ],
        compiler_params=pltpu.CompilerParams(
            collective_id=0, has_side_effects=True, vmem_limit_bytes=67043328
        ),
    )(blocks, filters, gain[None, :], doc_lengths)
    return out[None]


def solution(mesh):
    in_specs = (P("ctx", None, None, None, "dp"), P(None, None, "dp"), P("dp"), P())
    out_specs = P("ctx", None, None, "dp")
    return jax.shard_map(
        functools.partial(local, mesh.shape["ctx"], mesh.shape["dp"]),
        mesh=mesh,
        in_specs=in_specs,
        out_specs=out_specs,
        check_vma=False,
    )
```

```python
import functools
import math

import jax
import jax.numpy as jnp
from jax import lax
from jax.experimental import pallas as pl
from jax.experimental.pallas import tpu as pltpu
from jax.sharding import PartitionSpec as P

HEAD_DIM = 128
REACH = 5
RIM = 8
HEAD_ROWS = 16
PAIRS = (REACH + 1) // 2
LOG2_SCALE = HEAD_DIM ** (-0.5) * math.log2(math.e)
MESH = pl.DeviceIdType.MESH


def kernel(
    n_ctx,
    n_dp,
    x_ref,
    f_hbm,
    docs_hbm,
    out_ref,
    inv_norm,
    f_ref,
    docs_ref,
    parts,
    xs,
    xf,
    fw,
    halo,
    qb,
    kv,
    run_max,
    run_total,
    acc,
    squares,
    sq_own,
    sq_peer,
    starts,
    load_sem,
    out_sem,
    small_sem,
    halo_send,
    halo_recv,
    kv_send,
    kv_recv,
    sq_send,
    sq_recv,
):
    rows = xs.shape[2]
    width = xs.shape[3]
    groups = kv.shape[1]
    group_width = kv.shape[4]
    group_heads = group_width // HEAD_DIM
    taps = f_ref.shape[1]
    place = lax.axis_index("ctx")
    lane = lax.axis_index("dp")
    right = lax.rem(place + 1, n_ctx)
    left = lax.rem(place + n_ctx - 1, n_ctx)
    has_left = place > 0
    has_right = place < n_ctx - 1
    is_last = place == n_ctx - 1

    def load(g, b, first, count):
        lanes = pl.ds(g * group_width, group_width)
        return pltpu.make_async_copy(
            x_ref.at[b, pl.ds(first, count), :, lanes],
            xs.at[b, pl.ds(first, count), :, lanes],
            load_sem.at[b, min(first, 1), g],
        )

    def load_wait(g, b, first, count):
        lanes = pl.ds(pl.multiple_of(g * group_width, group_width), group_width)
        pltpu.make_async_copy(
            x_ref.at[b, pl.ds(first, count), :, lanes],
            xs.at[b, pl.ds(first, count), :, lanes],
            load_sem.at[b, min(first, 1), g],
        ).wait()

    load_small = [
        pltpu.make_async_copy(f_hbm, f_ref, small_sem.at[0]),
        pltpu.make_async_copy(docs_hbm, docs_ref, small_sem.at[1]),
    ]
    for copy in load_small:
        copy.start()
    for g in range(groups):
        for b in range(2):
            load(g, b, 1, 2).start()
    for g in range(groups):
        for b in range(2):
            load(g, b, 0, 1).start()

    barrier = pltpu.get_barrier_semaphore()

    @pl.when(has_left)
    def _():
        pl.semaphore_signal(barrier, inc=1, device_id={"ctx": left}, device_id_type=MESH)

    @pl.when(has_right)
    def _():
        pl.semaphore_signal(barrier, inc=1, device_id={"ctx": right}, device_id_type=MESH)

    for step in range(1, n_dp):
        peer = lax.rem(lane + step, n_dp)
        pl.semaphore_signal(barrier, inc=1, device_id={"dp": peer}, device_id_type=MESH)

    def rim(b, source, target):
        return pltpu.make_async_remote_copy(
            src_ref=x_ref.at[source, :, pl.ds(rows - RIM, RIM), :],
            dst_ref=halo.at[b],
            send_sem=halo_send.at[b],
            recv_sem=halo_recv.at[b],
            device_id={"ctx": target},
            device_id_type=MESH,
        )

    rim_lower = rim(0, 0, right)
    rim_upper = rim(1, 1, left)
    rim_fold = pltpu.make_async_copy(
        x_ref.at[0, :, pl.ds(rows - RIM, RIM), :], halo.at[1], halo_recv.at[1]
    )
    def channel(g, hl):
        return pl.ds(pl.multiple_of(g * group_width + hl * HEAD_DIM, HEAD_DIM), HEAD_DIM)

    spread_shape = (f_ref.shape[2], HEAD_DIM)
    spread_row = lax.broadcasted_iota(jnp.int32, spread_shape, 0)
    spread_col = lax.broadcasted_iota(jnp.int32, spread_shape, 1)
    group_size = width // f_ref.shape[2]
    parts[...] = jnp.zeros_like(parts)
    load_small[0].wait()
    for m in range(3):
        left_over = f_ref[m]
        for part in range(3):
            piece = left_over.astype(jnp.bfloat16).astype(jnp.float32)
            parts[3 * part + m, pl.ds(0, taps), :] = piece
            left_over = left_over - piece
    split = parts[...].reshape(72, f_ref.shape[2]).astype(jnp.bfloat16)

    def spread_taps(g):
        for hl in range(group_heads):
            first = g * group_width + hl * HEAD_DIM
            hot = (spread_row * group_size <= first + spread_col) & (
                first + spread_col < (spread_row + 1) * group_size
            )
            spread = jnp.dot(
                split,
                jnp.where(hot, 1.0, 0.0).astype(jnp.bfloat16),
                preferred_element_type=jnp.float32,
            ).reshape(9, 8, HEAD_DIM)
            for m in range(3):
                fw[m, :, channel(g, hl)] = (spread[m] + spread[3 + m]) + spread[6 + m]

    pl.semaphore_wait(barrier, n_dp - 1 + has_left.astype(jnp.int32) + has_right.astype(jnp.int32))

    @pl.when(has_right)
    def _():
        rim_lower.start()

    @pl.when(has_left)
    def _():
        rim_upper.start()

    @pl.when(is_last)
    def _():
        rim_fold.start()

    def convolved(b, m, lanes, first, count):
        total = None
        for s in range(taps):
            term = fw[m, pl.ds(s, 1), lanes] * xf[b, m, pl.ds(first + RIM - taps + 1 + s, count), lanes]
            total = term if total is None else total + term
        return total.astype(jnp.bfloat16)

    def inner(hl):
        return pl.ds(hl * HEAD_DIM, HEAD_DIM)

    def slot(b, g, d, first=0, count=rows):
        return kv.at[b, g, :, pl.ds(d * rows + first, count), :]

    def moved(b, g, d, target, first=0, count=rows):
        return pltpu.make_async_remote_copy(
            src_ref=slot(b, g, d - 1, first, count),
            dst_ref=slot(b, g, d, first, count),
            send_sem=kv_send.at[b, d - 1, g],
            recv_sem=kv_recv.at[b, d - 1, g],
            device_id={"ctx": target},
            device_id_type=MESH,
        )

    def folded(g, d):
        return pltpu.make_async_copy(slot(0, g, d - 1), slot(1, g, d), kv_recv.at[1, d - 1, g])

    def lower_sends(d):
        return has_right & (place + 1 >= d)

    def launch(g, d, first=0, count=rows):
        @pl.when(has_left)
        def _():
            moved(1, g, d, left, first, count).start()

        @pl.when(lower_sends(d))
        def _():
            moved(0, g, d, right, first, count).start()

        if first == 0:

            @pl.when(is_last)
            def _():
                folded(g, d).start()

    def arrive(g, d):
        @pl.when(place >= d)
        def _():
            moved(0, g, d, right).wait_recv()

        @pl.when(has_right)
        def _():
            moved(1, g, d, left).wait_recv()

        @pl.when(is_last)
        def _():
            folded(g, d).wait()

    def body_rows(g, carry):
        spread_taps(g)
        for b in range(2):
            load_wait(g, b, 1, 2)
        for b in range(2):
            for m in (1, 2):
                for hl in range(group_heads):
                    lanes = channel(g, hl)
                    xf[b, m, pl.ds(RIM, rows), lanes] = xs[b, m, :, lanes].astype(jnp.float32)
                for hl in range(group_heads):
                    kv[b, g, m - 1, pl.ds(HEAD_ROWS, rows - HEAD_ROWS), inner(hl)] = convolved(
                        b, m, channel(g, hl), HEAD_ROWS, rows - HEAD_ROWS
                    )
        launch(g, 1, HEAD_ROWS, rows - HEAD_ROWS)
        return carry

    lax.fori_loop(0, groups, body_rows, 0)

    @pl.when(place == 0)
    def _():
        halo[0] = jnp.zeros(halo.shape[1:], jnp.bfloat16)

    @pl.when(has_left)
    def _():
        rim_lower.wait_recv()

    @pl.when(has_right)
    def _():
        rim_upper.wait_recv()

    @pl.when(is_last)
    def _():
        rim_fold.wait()

    def first_rows(g, carry):
        for b in range(2):
            for m in (1, 2):
                for hl in range(group_heads):
                    lanes = channel(g, hl)
                    xf[b, m, pl.ds(0, RIM), lanes] = halo[b, m, :, lanes].astype(jnp.float32)
                    kv[b, g, m - 1, pl.ds(0, HEAD_ROWS), inner(hl)] = convolved(
                        b, m, lanes, 0, HEAD_ROWS
                    )
        launch(g, 1, 0, HEAD_ROWS)
        return carry

    lax.fori_loop(0, groups, first_rows, 0)

    for d in range(1, REACH + 1):

        @pl.when(place < d)
        def _():
            def clear(g, carry):
                kv[0, g, :, pl.ds(d * rows, rows), :] = jnp.zeros(
                    (2, rows, group_width), jnp.bfloat16
                )
                return carry

            lax.fori_loop(0, groups, clear, 0)

    load_small[1].wait()

    offsets = lax.broadcasted_iota(jnp.int32, (rows, HEAD_DIM), 0)
    block_start = [place * rows, (2 * n_ctx - 1 - place) * rows]
    for b in range(2):
        positions = block_start[b] + offsets

        def advance(k, carry):
            begin, end = carry
            end = end + docs_ref[k]
            return jnp.where(positions >= end, end, begin), end

        begin, _ = lax.fori_loop(
            0, docs_ref.shape[0], advance, (jnp.zeros_like(positions), jnp.int32(0))
        )
        starts[b] = begin

    def query_rows(g, carry):
        for b in range(2):
            load_wait(g, b, 0, 1)
            for hl in range(group_heads):
                lanes = channel(g, hl)
                xf[b, 0, pl.ds(0, RIM), lanes] = halo[b, 0, :, lanes].astype(jnp.float32)
                xf[b, 0, pl.ds(RIM, rows), lanes] = xs[b, 0, :, lanes].astype(jnp.float32)
            for hl in range(group_heads):
                qb[b, g, :, inner(hl)] = convolved(b, 0, channel(g, hl), 0, rows)
        return carry

    lax.fori_loop(0, groups, query_rows, 0)

    key_lane = lax.broadcasted_iota(jnp.int32, (rows, HEAD_DIM), 1)
    key_offset = jnp.where(key_lane >= rows, key_lane - 2 * rows, key_lane)
    span = 2 * rows

    def attend(pair, g):
        allowed = []
        for b in range(2):
            key_pos = key_offset + (block_start[b] - pair * span)
            allowed.append((key_pos >= starts[b]) & (key_pos <= block_start[b] + offsets))
        units = [(b, hl) for b in range(2) for hl in range(group_heads)]
        keys = pl.ds(pair * span, span)
        scores = [
            lax.dot_general(
                qb[b, g, :, inner(hl)],
                kv[b, g, 0, keys, inner(hl)],
                (((1,), (1,)), ((), ())),
                preferred_element_type=jnp.float32,
            )
            for b, hl in units
        ]
        scores = [
            jnp.where(allowed[b], score * LOG2_SCALE, -1e30)
            for score, (b, _) in zip(scores, units)
        ]
        tops = [jnp.max(score, axis=1, keepdims=True) for score in scores]
        if pair > 0:
            before = [run_max[b, g, hl] for b, hl in units]
            tops = [jnp.maximum(old, top) for old, top in zip(before, tops)]
        expos = [jnp.exp2(score - top) for score, top in zip(scores, tops)]
        updates = [
            jnp.dot(
                expo.astype(jnp.bfloat16),
                kv[b, g, 1, keys, inner(hl)],
                preferred_element_type=jnp.float32,
            )
            for expo, (b, hl) in zip(expos, units)
        ]
        totals = [jnp.sum(expo, axis=1, keepdims=True) for expo in expos]
        if pair > 0:
            rescales = [jnp.exp2(old - top) for old, top in zip(before, tops)]
            totals = [
                run_total[b, g, hl] * rescale + total
                for total, rescale, (b, hl) in zip(totals, rescales, units)
            ]
            updates = [
                acc[b, :, channel(g, hl)] * rescale + update
                for update, rescale, (b, hl) in zip(updates, rescales, units)
            ]
        if pair < PAIRS - 1:
            for top, total, update, (b, hl) in zip(tops, totals, updates, units):
                run_max[b, g, hl] = jnp.broadcast_to(top, (rows, HEAD_DIM))
                run_total[b, g, hl] = jnp.broadcast_to(total, (rows, HEAD_DIM))
                acc[b, :, channel(g, hl)] = update
        else:
            for total, update, (b, hl) in zip(totals, updates, units):
                attended = update / total
                acc[b, :, channel(g, hl)] = attended
                squares[pl.ds(b * rows, rows), :] += attended * attended

    squares[...] = jnp.zeros_like(squares)
    work = {2: 0, 4: 1}
    for d in range(1, REACH):

        def relay(g, carry):
            arrive(g, d)
            launch(g, d + 1)
            if d in work:
                attend(work[d], g)
            return carry

        lax.fori_loop(0, groups, relay, 0)

    def given(g, b):
        lanes = pl.ds(pl.multiple_of(g * group_width, group_width), group_width)
        return pltpu.make_async_copy(
            acc.at[b, :, lanes], out_ref.at[b, :, lanes], out_sem.at[b, g]
        )

    def finish(g, carry):
        arrive(g, REACH)
        attend(PAIRS - 1, g)
        for b in range(2):
            given(g, b).start()
        return carry

    lax.fori_loop(0, groups, finish, 0)

    row = jnp.sum(jnp.transpose(squares[...]), axis=0, keepdims=True)
    sq_own[...] = jnp.broadcast_to(row, sq_own.shape)
    shares = []
    for step in range(1, n_dp):
        share = pltpu.make_async_remote_copy(
            src_ref=sq_own,
            dst_ref=sq_peer.at[step - 1],
            send_sem=sq_send.at[step - 1],
            recv_sem=sq_recv.at[step - 1],
            device_id={"dp": lax.rem(lane + step, n_dp)},
            device_id_type=MESH,
        )
        share.start()
        shares.append(share)

    @pl.when(has_right)
    def _():
        rim_lower.wait_send()

    @pl.when(has_left)
    def _():
        rim_upper.wait_send()

    for d in range(1, REACH + 1):

        def drain(g, carry):
            @pl.when(has_left)
            def _():
                moved(1, g, d, left).wait_send()

            @pl.when(lower_sends(d))
            def _():
                moved(0, g, d, right).wait_send()

            return carry

        lax.fori_loop(0, groups, drain, 0)

    whole = sq_own[...]
    for step in range(1, n_dp):
        shares[step - 1].wait()
        whole = whole + sq_peer[step - 1]
    inverse = lax.rsqrt(whole / (width * n_dp) + 1e-06)
    inv_norm[...] = jnp.transpose(jnp.broadcast_to(inverse[0:1], inv_norm.shape))

    def settle(g, carry):
        for b in range(2):
            given(g, b).wait()
        return carry

    lax.fori_loop(0, groups, settle, 0)


def local(n_ctx, n_dp, projected, filters, gain, doc_lengths):
    blocks = jnp.transpose(projected[0], (0, 2, 1, 3))
    rows, width = blocks.shape[2], blocks.shape[3]
    group_width = min(width, 2 * HEAD_DIM)
    groups = width // group_width
    group_heads = group_width // HEAD_DIM
    vmem = pl.BlockSpec(memory_space=pltpu.VMEM)
    attended, inverse = pl.pallas_call(
        functools.partial(kernel, n_ctx, n_dp),
        out_shape=(
            jax.ShapeDtypeStruct((2, rows, width), jnp.float32),
            jax.ShapeDtypeStruct((2 * rows, HEAD_DIM), jnp.float32),
        ),
        in_specs=[
            pl.BlockSpec(memory_space=pltpu.HBM),
            pl.BlockSpec(memory_space=pltpu.HBM),
            pl.BlockSpec(memory_space=pltpu.HBM),
        ],
        out_specs=(pl.BlockSpec(memory_space=pltpu.HBM), vmem),
        scratch_shapes=[
            pltpu.VMEM(filters.shape, jnp.float32),
            pltpu.SMEM(doc_lengths.shape, jnp.int32),
            pltpu.VMEM((9, 8, filters.shape[2]), jnp.float32),
            pltpu.VMEM((2, 3, rows, width), jnp.bfloat16),
            pltpu.VMEM((2, 3, RIM + rows, width), jnp.float32),
            pltpu.VMEM((3, 8, width), jnp.float32),
            pltpu.VMEM((2, 3, RIM, width), jnp.bfloat16),
            pltpu.VMEM((2, groups, rows, group_width), jnp.bfloat16),
            pltpu.VMEM((2, groups, 2, (REACH + 1) * rows, group_width), jnp.bfloat16),
            pltpu.VMEM((2, groups, group_heads, rows, HEAD_DIM), jnp.float32),
            pltpu.VMEM((2, groups, group_heads, rows, HEAD_DIM), jnp.float32),
            pltpu.VMEM((2, rows, width), jnp.float32),
            pltpu.VMEM((2 * rows, HEAD_DIM), jnp.float32),
            pltpu.VMEM((8, 2 * rows), jnp.float32),
            pltpu.VMEM((n_dp - 1, 8, 2 * rows), jnp.float32),
            pltpu.VMEM((2, rows, HEAD_DIM), jnp.int32),
            pltpu.SemaphoreType.DMA((2, 2, groups)),
            pltpu.SemaphoreType.DMA((2, groups)),
            pltpu.SemaphoreType.DMA((2,)),
            pltpu.SemaphoreType.DMA((2,)),
            pltpu.SemaphoreType.DMA((2,)),
            pltpu.SemaphoreType.DMA((2, REACH, groups)),
            pltpu.SemaphoreType.DMA((2, REACH, groups)),
            pltpu.SemaphoreType.DMA((n_dp - 1,)),
            pltpu.SemaphoreType.DMA((n_dp - 1,)),
        ],
        compiler_params=pltpu.CompilerParams(
            collective_id=0, has_side_effects=True, vmem_limit_bytes=67043328
        ),
    )(blocks, filters, doc_lengths)
    inverse = inverse.reshape(2, rows, HEAD_DIM)[:, :, :1]
    return (attended * inverse * gain).astype(jnp.bfloat16)[None]


def solution(mesh):
    in_specs = (P("ctx", None, None, None, "dp"), P(None, None, "dp"), P("dp"), P())
    out_specs = P("ctx", None, None, "dp")
    return jax.shard_map(
        functools.partial(local, mesh.shape["ctx"], mesh.shape["dp"]),
        mesh=mesh,
        in_specs=in_specs,
        out_specs=out_specs,
        check_vma=False,
    )
```
